256 devices in a mesh: blk: 32 (over x_hi, z, core), ang: 8 (over x_lo, y).
Axes of the slice: x: 4 (x_hi: 2, x_lo: 2; x = x_hi * 2 + x_lo), y: 4, z: 8, core: 2. Of those that a mesh axis runs over, the one named last changes fastest.
Arguments:
- coeffs: bfloat16 [8192, 2048], P('blk'), may hold values from -6 to 6
- orders: int32 [1024], replicated, may hold values from 0 to 47
- plan: int32 [2], replicated, may hold values from 1 to 31
Outputs:
- scores: float32 [2, 8192, 256], P(None, ('blk', 'ang'))
The draws below stay inside these ranges and needn't reach their ends.
Inputs may be any that keep to these rules, and one draw needn't show every extreme that they name: In round r, block b is paired with block b XOR plan[r].
All inputs are finite; a program needn't handle non-finite values.
Results may differ from the reference program's by a relative error of at most 0.002.
Values may be sent and summed in bfloat16 or wider, within the bound.
No kernel may reach another device: no remote copies, remote signals or barrier semaphores. Data moves between devices by JAX's collectives and lax.ppermute only.
A program may use at most 64 MiB of HBM per device.

```python
import math
import jax
import jax.numpy as jnp
from jax import lax

IMG_DEV = 256
COEF = 2048
ANGLES = 128
ORDERS = 48
ROUNDS = 2
HALF = 1024
IMAGES = 8192
N_BLK = 32


def with_ends(entries, stream_key, least, high):
    longest = entries.shape.index(max(entries.shape))
    spots = []
    for shift in (0, 1):
        where = [jax.random.randint(jax.random.fold_in(stream_key, axis), (), 0, length) for axis, length in enumerate(entries.shape)]
        where[longest] = (where[longest] + shift) % entries.shape[longest]
        spots.append(tuple(where))
    return entries.at[spots[0]].set(least).at[spots[1]].set(high)


def shard_levels(key, extent, pieces, smallest, largest):
    level, own = 1.0, jax.random.fold_in(key, 6)
    for axis_at, parts in pieces:
        draws = jnp.exp(jax.random.uniform(jax.random.fold_in(own, axis_at), (parts,), jnp.float32, smallest / len(pieces), largest / len(pieces)))
        level = level * jnp.repeat(draws, extent[axis_at] // parts).reshape([-1 if axis == axis_at else 1 for axis in range(len(extent))])
    return level


def normal_values(rng, extent, deviation, reach, pieces=(), kind=jnp.bfloat16):
    loudness = shard_levels(rng, extent, pieces, -0.22, 0.18) if pieces else 1.0
    array = jax.random.normal(rng, extent, jnp.float32) * deviation * loudness
    return jnp.minimum(jnp.maximum(array, -reach), reach).astype(kind)


def setup_inputs(seed: int = 0) -> dict:
    key_of = jax.random.split(jax.random.key(seed), 4)
    return {
        "coeffs": normal_values(key_of[0], (IMAGES, COEF), 1.0, 6.0, ((0, 32),)),
        "orders": with_ends(jax.random.randint(key_of[1], (HALF,), 0, ORDERS), jax.random.fold_in(key_of[1], 1), 0, ORDERS - 1).astype(jnp.int32),
        "plan": jax.random.randint(key_of[2], (ROUNDS,), 1, N_BLK).astype(jnp.int32),
    }


def rotate_rows(block, orders, first_angle, angle_count):
    half_width = block.shape[1] // 2
    real_part = block[:, :half_width].astype(jnp.float32)
    imag_part = block[:, half_width:].astype(jnp.float32)
    angles = (jnp.arange(angle_count) + first_angle).astype(jnp.float32) * (2.0 * math.pi / ANGLES)
    phases = angles[:, None] * orders.astype(jnp.float32)[None, :]
    cosine_table = jnp.cos(phases)[:, None, :]
    sine_table = jnp.sin(phases)[:, None, :]
    rot_real = real_part[None] * cosine_table - imag_part[None] * sine_table
    rot_imag = real_part[None] * sine_table + imag_part[None] * cosine_table
    return jnp.concatenate([rot_real, rot_imag], axis=2).astype(jnp.bfloat16)

def block_best(own_block, partner, orders):
    group_size = 8
    row_count = own_block.shape[0]
    partner_wide = partner.astype(jnp.float32)

    def step(running, step_index):
        rotated = rotate_rows(own_block, orders, step_index * group_size, group_size).astype(jnp.float32)
        stacked = rotated.reshape(group_size * row_count, -1)
        scores_raw = jnp.dot(stacked, partner_wide.T, precision=lax.Precision.HIGHEST, preferred_element_type=jnp.float32)
        return (jnp.maximum(running, scores_raw.reshape(group_size, row_count, -1).max(0)), None)
    start = jnp.full((row_count, partner.shape[0]), -jnp.inf, jnp.float32)
    running, _ = lax.scan(step, start, jnp.arange(ANGLES // group_size, dtype=jnp.int32))
    return running

def reference(coeffs, orders, plan):
    blocks = coeffs.reshape(N_BLK, IMG_DEV, COEF)
    scales = jnp.sqrt(lax.optimization_barrier(jnp.mean(jnp.square(coeffs.astype(jnp.float32)), axis=1)) + 1e-06).reshape(N_BLK, IMG_DEV)
    block_ids = jnp.arange(N_BLK, dtype=jnp.int32)
    round_scores = []
    for round_index in range(ROUNDS):
        partner_ids = jnp.bitwise_xor(block_ids, plan[round_index])

        def per_block(block_index):
            mate = partner_ids[block_index]
            running = block_best(blocks[block_index], blocks[mate], orders)
            return running / (math.sqrt(COEF) * scales[block_index][:, None] * scales[mate][None, :])
        round_scores.append(lax.map(per_block, block_ids).reshape(IMAGES, IMG_DEV))
    return jnp.stack(round_scores)
```

```python
import math

import jax
import jax.numpy as jnp
from jax import lax
from jax.sharding import PartitionSpec as P

ANGLES = 128
ROUNDS = 2


def from_block(rows, offset, blocks):
    def moved(apart):
        pairs = [(source, source ^ apart) for source in range(blocks)]
        return lambda piece: lax.ppermute(piece, "blk", pairs)

    return lax.switch(offset - 1, [moved(apart) for apart in range(1, blocks)], rows)


def rotate_rows(block, orders, first_angle, angle_count):
    half_width = block.shape[1] // 2
    real_part = block[:, :half_width].astype(jnp.float32)
    imag_part = block[:, half_width:].astype(jnp.float32)
    angles = (jnp.arange(angle_count) + first_angle).astype(jnp.float32) * (2.0 * math.pi / ANGLES)
    phases = angles[:, None] * orders.astype(jnp.float32)[None, :]
    cosine_table = jnp.cos(phases)[:, None, :]
    sine_table = jnp.sin(phases)[:, None, :]
    rot_real = real_part[None] * cosine_table - imag_part[None] * sine_table
    rot_imag = real_part[None] * sine_table + imag_part[None] * cosine_table
    return jnp.concatenate([rot_real, rot_imag], axis=2).astype(jnp.bfloat16)


def group_width(angle_count, row_count):
    group_size = 1
    while (
        group_size * 2 <= angle_count
        and angle_count % (group_size * 2) == 0
        and (group_size * 2 * row_count <= 512)
    ):
        group_size = group_size * 2
    return group_size


def angle_best(own_rows, partner, orders, first_angle, angle_count):
    row_count = own_rows.shape[0]
    group_size = group_width(angle_count, row_count)

    def step(step_index, running):
        rotated = rotate_rows(own_rows, orders, first_angle + step_index * group_size, group_size)
        stacked = rotated.reshape(group_size * row_count, -1)
        scores_raw = lax.dot_general(
            stacked, partner, (((1,), (1,)), ((), ())), preferred_element_type=jnp.float32
        )
        return jnp.maximum(running, scores_raw.reshape(group_size, row_count, -1).max(0))

    start = jnp.full((row_count, partner.shape[0]), -jnp.inf, jnp.float32)
    return lax.fori_loop(0, angle_count // group_size, step, start)


def per_device(coeffs, orders, plan):
    ang_count = lax.axis_size("ang")
    ang_index = lax.axis_index("ang")
    blocks = lax.axis_size("blk")
    row_count, col_width = coeffs.shape
    share = row_count // ang_count
    scales = jnp.sqrt(jnp.mean(jnp.square(coeffs.astype(jnp.float32)), axis=1) + 1e-06)
    own_rows = lax.dynamic_slice_in_dim(coeffs, ang_index * share, share, 0)
    results = []
    for round_index in range(ROUNDS):
        rows = from_block(own_rows, plan[round_index], blocks)
        row_scales = jnp.sqrt(jnp.mean(jnp.square(rows.astype(jnp.float32)), axis=1) + 1e-06)
        best = angle_best(rows, coeffs, orders, 0, ANGLES)
        results.append(best / (math.sqrt(col_width) * row_scales[:, None] * scales[None, :]))
    both = jnp.stack(results).reshape(ROUNDS, share, ang_count, share)
    pieces = lax.all_to_all(both.transpose(2, 0, 3, 1), "ang", 0, 0, tiled=True)
    return pieces.transpose(1, 2, 0, 3).reshape(ROUNDS, share, row_count)


def solution(mesh):
    in_specs = (P("blk", None), P(), P())
    out_specs = P(None, ("blk", "ang"), None)
    return jax.shard_map(
        per_device, mesh=mesh, in_specs=in_specs, out_specs=out_specs, check_vma=False
    )
```

```python
import functools
import math

import jax
import jax.numpy as jnp
from jax import lax
from jax.experimental import pallas as pl
from jax.experimental.pallas import tpu as pltpu
from jax.sharding import PartitionSpec as P

ANGLES = 128
ORDERS = 48
ROUNDS = 2
LANES = 128
GROUP = 4


def plus(u, v):
    if u is None or v is None:
        return u if v is None else v
    (su, a), (sv, b) = u, v
    if su == sv:
        return (su, a + b)
    return (1, a - b) if su > 0 else (1, b - a)


def negative(u):
    return None if u is None else (-u[0], u[1])


def minus(u, v):
    return plus(u, negative(v))


def times(u, factor):
    return None if u is None else (u[0], u[1] * jnp.float32(factor))


def plain(u):
    return u[1] if u[0] > 0 else -u[1]


def cosine_sums(x):
    size = len(x)
    if size == 1:
        return [x[0]]
    half = size // 2
    even = cosine_sums([plus(x[n], x[size - 1 - n]) for n in range(half)])
    odd = cosine_sums(
        [
            times(minus(x[n], x[size - 1 - n]), 2.0 * math.cos(math.pi * (2 * n + 1) / (2 * size)))
            for n in range(half)
        ]
    )
    out = [None] * size
    for a in range(half):
        out[2 * a] = even[a]
        out[2 * a + 1] = times(odd[0], 0.5) if a == 0 else minus(odd[a], out[2 * a - 1])
    return out


def padded(x, size):
    return x + [None] * (size - len(x))


def cosine_series(terms, period):
    if len(terms) == 1:
        return [terms[0]] * (period // 2 + 1)
    quarter = period // 4
    even = cosine_series(terms[0::2], period // 2)
    odd = cosine_sums(padded(terms[1::2], quarter)) + [None]
    out = [None] * (period // 2 + 1)
    for a in range(quarter + 1):
        out[a] = plus(even[a], odd[a])
        out[period // 2 - a] = minus(even[a], odd[a])
    return out


def sine_series(terms, period):
    if len(terms) == 1:
        return [None] * (period // 2 + 1)
    quarter = period // 4
    even = sine_series(terms[0::2], period // 2)
    flipped = [u if n % 2 == 0 else negative(u) for n, u in enumerate(terms[1::2])]
    odd = [None] + cosine_sums(padded(flipped, quarter))[::-1]
    out = [None] * (period // 2 + 1)
    for a in range(quarter + 1):
        out[period // 2 - a] = minus(odd[a], even[a])
        out[a] = plus(even[a], odd[a])
    return out


def best_angle(cosine_terms, sine_terms):
    across = cosine_series([(1, u) for u in cosine_terms], ANGLES)
    along = sine_series([(1, u) for u in sine_terms], ANGLES)
    best = None
    for u, v in zip(across, along, strict=True):
        value = plain(u)
        if v is not None:
            value = value + jnp.abs(v[1])
        best = value if best is None else jnp.maximum(best, value)
    return best


def scale_of(rows):
    wide = rows.astype(jnp.float32)
    return jnp.sqrt(jnp.mean(wide * wide, axis=1, keepdims=True) + 1e-06)


def prepare_kernel(own_ref, orders_ref, sorted_ref, places_ref, order_ref, scale_ref, select):
    half = orders_ref.shape[1]
    images = own_ref.shape[0]
    keys = orders_ref[...] * half + lax.broadcasted_iota(jnp.int32, (1, half), 1)
    keys = keys.astype(jnp.float32)
    keys_down = jnp.transpose(jnp.broadcast_to(keys, (LANES, half)))
    for c in range(half // LANES):
        rows = slice(c * LANES, (c + 1) * LANES)
        ahead = jnp.where(keys < keys_down[rows, :1], 1.0, 0.0)
        place = jnp.sum(ahead, axis=1, keepdims=True)
        places_ref[rows, :] = jnp.broadcast_to(place, (LANES, LANES)).astype(jnp.int32)
    fill_select(places_ref, select)
    order = jnp.dot(
        jnp.broadcast_to(orders_ref[...].astype(jnp.float32), (16, half)).astype(jnp.bfloat16),
        select[...],
        preferred_element_type=jnp.float32,
    )[:1]
    for t in range(half // LANES):
        part = order[:, t * LANES : (t + 1) * LANES].astype(jnp.int32)
        order_ref[:, 2 * t * LANES : (2 * t + 1) * LANES] = part
        order_ref[:, (2 * t + 1) * LANES : (2 * t + 2) * LANES] = part
    for side in range(2):
        moved = jnp.dot(
            own_ref[:, side * half : (side + 1) * half],
            select[...],
            preferred_element_type=jnp.float32,
        ).astype(jnp.bfloat16)
        for t in range(half // LANES):
            sorted_ref[:, (2 * t + side) * LANES : (2 * t + side + 1) * LANES] = moved[
                :, t * LANES : (t + 1) * LANES
            ]
    scale = scale_of(own_ref[...])
    scale_ref[...] = jnp.transpose(jnp.broadcast_to(scale, (images, LANES)))[:8]


def fill_select(places_ref, select):
    half = select.shape[0]
    for c in range(half // LANES):
        rows = slice(c * LANES, (c + 1) * LANES)
        lane = lax.broadcasted_iota(jnp.int32, (LANES, half), 1)
        hit = lane == places_ref[rows, :1]
        select[rows, :] = jnp.where(hit, 1.0, 0.0).astype(jnp.bfloat16)


def score_kernel(
    first_ref, second_ref, own_ref, places_ref, order_ref, scale_ref, out_ref, select, pair, terms, best
):
    half = select.shape[0]
    tiles = half // LANES
    share = first_ref.shape[0]
    images = own_ref.shape[0]
    rows = 2 * ROUNDS * share
    inputs = (first_ref, second_ref)
    fill_select(places_ref, select)
    terms[...] = jnp.zeros_like(terms)
    stacked = jnp.concatenate(
        [ref[:, side * half : (side + 1) * half] for ref in inputs for side in range(2)], axis=0
    )
    moved = jnp.dot(stacked, select[...], preferred_element_type=jnp.float32)
    for r in range(ROUNDS):
        x = moved[2 * r * share : (2 * r + 1) * share]
        y = moved[(2 * r + 1) * share : (2 * r + 2) * share]
        up, down = slice(2 * r * share, (2 * r + 1) * share), slice((2 * r + 1) * share, (2 * r + 2) * share)
        for t in range(tiles):
            one, two = slice(2 * t * LANES, (2 * t + 1) * LANES), slice((2 * t + 1) * LANES, (2 * t + 2) * LANES)
            xt, yt = x[:, t * LANES : (t + 1) * LANES], y[:, t * LANES : (t + 1) * LANES]
            pair[up, one] = xt.astype(jnp.bfloat16)
            pair[up, two] = yt.astype(jnp.bfloat16)
            pair[down, one] = yt.astype(jnp.bfloat16)
            pair[down, two] = (-xt).astype(jnp.bfloat16)

    for t in range(tiles):
        cols = slice(2 * t * LANES, (2 * t + 2) * LANES)
        here = order_ref[:, cols]
        least, most = jnp.min(here), jnp.max(here)

        def step(c, _, cols=cols, here=here, least=least):
            base = least + GROUP * c
            block = pair[:, cols]
            masked = jnp.concatenate(
                [block * jnp.where(here == base + q, 1.0, 0.0).astype(jnp.bfloat16) for q in range(GROUP)],
                axis=0,
            )
            found = lax.dot_general(
                masked, own_ref[:, cols], (((1,), (1,)), ((), ())), preferred_element_type=jnp.float32
            )
            at = pl.ds(pl.multiple_of(base * rows, rows), GROUP * rows)
            terms[at, :] += found
            return 0

        lax.fori_loop(0, (most - least) // GROUP + 1, step, 0)

    wide = images // LANES

    def block(n, _):
        lane = pl.ds(pl.multiple_of(lax.rem(n, wide) * LANES, LANES), LANES)
        group = n // wide
        r = group // (share // 8)
        j = lax.rem(group, share // 8)
        start = r * 2 * share + j * 8
        cosine_terms = [terms[pl.ds(pl.multiple_of(m * rows + start, 8), 8), lane] for m in range(ORDERS)]
        sine_terms = [
            terms[pl.ds(pl.multiple_of(m * rows + start + share, 8), 8), lane] for m in range(ORDERS)
        ]
        best[pl.ds(pl.multiple_of(group * 8, 8), 8), lane] = best_angle(cosine_terms, sine_terms)
        return 0

    lax.fori_loop(0, ROUNDS * (share // 8) * wide, block, 0)
    scales = jnp.concatenate([scale_of(ref[...]) for ref in inputs], axis=0)
    value = best[...] / (math.sqrt(2 * half) * scales * scale_ref[:1, :])
    fill = jnp.zeros((LANES - ROUNDS * share, images), jnp.float32)
    turned = jnp.transpose(jnp.concatenate([value, fill], axis=0))
    lane = lax.broadcasted_iota(jnp.int32, (share // 2, LANES), 1)
    for g in range(images // share):
        top = turned[g * share : g * share + share // 2]
        low = pltpu.roll(turned[g * share + share // 2 : (g + 1) * share], LANES // 2, 1)
        out_ref[g] = jnp.where(lane < LANES // 2, top, low)


def place_kernel(pieces_ref, out_ref):
    count, short, _ = pieces_ref.shape
    share = 2 * short
    lane = lax.broadcasted_iota(jnp.int32, (short, LANES), 1)
    for r in range(ROUNDS):
        for h in range(2):
            for column in range(count * share // LANES):
                whole = None
                for k in range(LANES // share):
                    shift = (k * share - h * (LANES // 2) - r * share) % LANES
                    piece = pieces_ref[column * (LANES // share) + k]
                    piece = pltpu.roll(piece, shift, 1) if shift else piece
                    whole = piece if whole is None else jnp.where(lane < k * share, whole, piece)
                out_ref[r, h * short : (h + 1) * short, column * LANES : (column + 1) * LANES] = whole


VMEM = pl.BlockSpec(memory_space=pltpu.VMEM)


def call(kernel, inputs, shapes, scratch=(), flops=0):
    return pl.pallas_call(
        kernel,
        out_shape=shapes,
        in_specs=[VMEM] * len(inputs),
        out_specs=jax.tree.map(lambda _: VMEM, shapes),
        scratch_shapes=list(scratch),
        compiler_params=pltpu.CompilerParams(vmem_limit_bytes=48 * 2**20),
        cost_estimate=pl.CostEstimate(flops=flops, bytes_accessed=2**21, transcendentals=0),
    )(*inputs)


def from_chip(rows, offset, chips):
    def moved(apart):
        pairs = [(source, source ^ (2 * apart)) for source in range(2 * chips)]
        return lambda piece: lax.ppermute(piece, "blk", pairs)

    return lax.switch(offset, [lambda piece: piece] + [moved(apart) for apart in range(1, chips)], rows)


def per_device(coeffs, orders, plan):
    ang_count = lax.axis_size("ang")
    ang_index = lax.axis_index("ang")
    blocks = lax.axis_size("blk")
    images, width = coeffs.shape
    half = width // 2
    share = images // ang_count
    f32, bf16, i32 = jnp.float32, jnp.bfloat16, jnp.int32
    shape = jax.ShapeDtypeStruct

    own_rows = lax.dynamic_slice_in_dim(coeffs, ang_index * share, share, 0)
    other_rows = lax.ppermute(own_rows, "blk", [(source, source ^ 1) for source in range(blocks)])
    own_sorted, places, order, scale = call(
        prepare_kernel,
        (coeffs, orders.reshape(1, half)),
        (
            shape((images, width), bf16),
            shape((half, LANES), i32),
            shape((1, width), i32),
            shape((8, images), f32),
        ),
        [pltpu.VMEM((half, half), bf16)],
        flops=2 * images * width * half,
    )
    partner = []
    for r in range(ROUNDS):
        crossed = (plan[r] & 1) == 1
        sent = jnp.where(crossed, other_rows, own_rows)
        partner.append(from_chip(sent, plan[r] >> 1, blocks // 2))
    rows = 2 * ROUNDS * share
    pieces = call(
        score_kernel,
        (*partner, own_sorted, places, order, scale),
        shape((ang_count, share // 2, LANES), f32),
        [
            pltpu.VMEM((half, half), bf16),
            pltpu.VMEM((rows, width), bf16),
            pltpu.VMEM(((ORDERS + GROUP) * rows, images), f32),
            pltpu.VMEM((ROUNDS * share, images), f32),
        ],
        flops=2 * images * width * rows * 4,
    )
    pieces = lax.all_to_all(pieces, "ang", 0, 0, tiled=True)
    return call(place_kernel, (pieces,), shape((ROUNDS, share, images), f32))


def solution(mesh):
    in_specs = (P("blk", None), P(), P())
    out_specs = P(None, ("blk", "ang"), None)
    return jax.shard_map(
        per_device, mesh=mesh, in_specs=in_specs, out_specs=out_specs, check_vma=False
    )
```

```python
import functools
import math

import jax
import jax.numpy as jnp
from jax import lax
from jax.experimental import pallas as pl
from jax.experimental.pallas import tpu as pltpu
from jax.sharding import PartitionSpec as P

ANGLES = 128
ORDERS = 48
ROUNDS = 2
LANES = 128
GROUP = 8


def plus(u, v):
    if u is None or v is None:
        return u if v is None else v
    (su, a), (sv, b) = u, v
    if su == sv:
        return (su, a + b)
    return (1, a - b) if su > 0 else (1, b - a)


def negative(u):
    return None if u is None else (-u[0], u[1])


def minus(u, v):
    return plus(u, negative(v))


def times(u, factor):
    return None if u is None else (u[0], u[1] * jnp.float32(factor))


def plain(u):
    return u[1] if u[0] > 0 else -u[1]


def cosine_sums(x):
    size = len(x)
    if size == 1:
        return [x[0]]
    half = size // 2
    even = cosine_sums([plus(x[n], x[size - 1 - n]) for n in range(half)])
    odd = cosine_sums(
        [
            times(minus(x[n], x[size - 1 - n]), 2.0 * math.cos(math.pi * (2 * n + 1) / (2 * size)))
            for n in range(half)
        ]
    )
    out = [None] * size
    for a in range(half):
        out[2 * a] = even[a]
        out[2 * a + 1] = times(odd[0], 0.5) if a == 0 else minus(odd[a], out[2 * a - 1])
    return out


def padded(x, size):
    return x + [None] * (size - len(x))


def cosine_series(terms, period):
    if len(terms) == 1:
        return [terms[0]] * (period // 2 + 1)
    quarter = period // 4
    even = cosine_series(terms[0::2], period // 2)
    odd = cosine_sums(padded(terms[1::2], quarter)) + [None]
    out = [None] * (period // 2 + 1)
    for a in range(quarter + 1):
        out[a] = plus(even[a], odd[a])
        out[period // 2 - a] = minus(even[a], odd[a])
    return out


def sine_series(terms, period):
    if len(terms) == 1:
        return [None] * (period // 2 + 1)
    quarter = period // 4
    even = sine_series(terms[0::2], period // 2)
    flipped = [u if n % 2 == 0 else negative(u) for n, u in enumerate(terms[1::2])]
    odd = [None] + cosine_sums(padded(flipped, quarter))[::-1]
    out = [None] * (period // 2 + 1)
    for a in range(quarter + 1):
        out[period // 2 - a] = minus(odd[a], even[a])
        out[a] = plus(even[a], odd[a])
    return out


def best_angle(cosine_terms, sine_terms):
    across = cosine_series([(1, u) for u in cosine_terms], ANGLES)
    along = sine_series([(1, u) for u in sine_terms], ANGLES)
    best = None
    for u, v in zip(across, along, strict=True):
        value = plain(u)
        if v is not None:
            value = value + jnp.abs(v[1])
        best = value if best is None else jnp.maximum(best, value)
    return best


def scale_of(rows):
    wide = rows.astype(jnp.float32)
    return jnp.sqrt(jnp.mean(wide * wide, axis=1, keepdims=True) + 1e-06)


def prepare_kernel(
    own_hbm, orders_hbm, plan_hbm, first_ref, second_ref, turned_ref, rows_ref, order_ref, ends_ref, scale_ref,
    own, orders, plan, select, gathered, arrived
):
    half = orders.shape[1]
    images = own.shape[0]
    share = rows_ref.shape[0]
    tiles = half // LANES
    copies = [
        pltpu.make_async_copy(source, target, arrived.at[n])
        for n, (source, target) in enumerate(((orders_hbm, orders), (plan_hbm, plan), (own_hbm, own)))
    ]
    for copy in copies:
        copy.start()
    copies[0].wait()
    keys = orders[...] * half + lax.broadcasted_iota(jnp.int32, (1, half), 1)
    keys = keys.astype(jnp.float32)
    keys_down = jnp.transpose(jnp.broadcast_to(keys, (LANES, half)))
    place = jnp.zeros((1, half), jnp.float32)
    for c in range(tiles):
        behind = keys_down[c * LANES : (c + 1) * LANES, :1] < keys
        place = place + jnp.sum(jnp.where(behind, 1.0, 0.0), axis=0, keepdims=True)
    place = jnp.transpose(jnp.broadcast_to(place, (LANES, half))).astype(jnp.int32)
    spot = lax.broadcasted_iota(jnp.int32, (LANES, half), 1)
    for c in range(tiles):
        rows = slice(c * LANES, (c + 1) * LANES)
        select[rows, :] = jnp.where(spot == place[rows, :1], 1.0, 0.0).astype(jnp.bfloat16)
    wide = jnp.broadcast_to(orders[...].astype(jnp.float32), (16, half)).astype(jnp.bfloat16)
    order = jnp.dot(wide, select[...], preferred_element_type=jnp.float32)[:1].astype(jnp.int32)
    for t in range(tiles):
        part = order[:, t * LANES : (t + 1) * LANES]
        order_ref[:, 2 * t * LANES : (2 * t + 1) * LANES] = part
        order_ref[:, (2 * t + 1) * LANES : (2 * t + 2) * LANES] = part
        ends_ref[2 * t] = jnp.min(part)
        ends_ref[2 * t + 1] = jnp.max(part)
    copies[1].wait()
    first_ref[0] = lax.shift_right_logical(plan[0], 1)
    second_ref[0] = lax.shift_right_logical(plan[1], 1)
    copies[2].wait()
    for side in range(2):
        moved = jnp.dot(
            own[:, side * half : (side + 1) * half], select[...], preferred_element_type=jnp.float32
        ).astype(jnp.bfloat16)
        for t in range(tiles):
            there = slice((2 * t + side) * LANES, (2 * t + side + 1) * LANES)
            part = moved[:, t * LANES : (t + 1) * LANES]
            gathered[:, there] = part
            turned_ref[there, :] = jnp.transpose(part)
    mine = pl.ds(pl.multiple_of(lax.axis_index("ang") * share, share), share)
    rows_ref[...] = gathered[mine, :]
    scale_ref[...] = jnp.transpose(jnp.broadcast_to(scale_of(own[...]), (images, LANES)))[:8]


def choose_kernel(plan_ref, own_ref, other_ref, first_ref, second_ref):
    for r, ref in enumerate((first_ref, second_ref)):
        crossed = (plan_ref[r] & 1) == 1

        @pl.when(crossed)
        def _(ref=ref):
            ref[...] = other_ref[...]

        @pl.when(jnp.logical_not(crossed))
        def _(ref=ref):
            ref[...] = own_ref[...]


def add_tile(cols, base, order_ref, turned_ref, pair, terms):
    rows = pair.shape[0]
    here, block = order_ref[:, cols], pair[:, cols]
    masked = jnp.concatenate(
        [block * jnp.where(here == base + q, 1.0, 0.0).astype(jnp.bfloat16) for q in range(GROUP)], axis=0
    )
    found = jnp.dot(masked, turned_ref[cols, :], preferred_element_type=jnp.float32)
    terms[pl.ds(pl.multiple_of(base * rows, rows), GROUP * rows), :] += found


def round_scores(straight, rows_ref, turned_ref, order_ref, ends_ref, scale_ref, best, pair, terms):
    share, width = rows_ref.shape
    images = turned_ref.shape[1]
    tiles = width // (2 * LANES)
    rows = 2 * share
    terms[...] = jnp.zeros_like(terms)
    for t in range(tiles):
        one = slice(2 * t * LANES, (2 * t + 1) * LANES)
        two = slice((2 * t + 1) * LANES, (2 * t + 2) * LANES)
        x, y = rows_ref[:, one], rows_ref[:, two]
        pair[:share, one] = x
        pair[:share, two] = y
        pair[share:, one] = y
        pair[share:, two] = -x

    if straight:
        for t in range(tiles):
            cols = slice(2 * t * LANES, (2 * t + 2) * LANES)
            add_tile(cols, ends_ref[2 * t], order_ref, turned_ref, pair, terms)

    def tile(t, _):
        least, most = ends_ref[2 * t], ends_ref[2 * t + 1]
        cols = pl.ds(pl.multiple_of(2 * t * LANES, 2 * LANES), 2 * LANES)

        def step(c, _):
            add_tile(cols, least + GROUP * c, order_ref, turned_ref, pair, terms)
            return 0

        return lax.fori_loop(1 if straight else 0, (most - least) // GROUP + 1, step, 0)

    lax.fori_loop(0, tiles, tile, 0)
    wide = images // LANES

    def block(n, _):
        lane = pl.ds(pl.multiple_of(lax.rem(n, wide) * LANES, LANES), LANES)
        j = pl.multiple_of(n // wide * 8, 8)
        cosine_terms = [terms[pl.ds(m * rows + j, 8), lane] for m in range(ORDERS)]
        sine_terms = [terms[pl.ds(m * rows + share + j, 8), lane] for m in range(ORDERS)]
        best[pl.ds(j, 8), lane] = best_angle(cosine_terms, sine_terms)
        return 0

    lax.fori_loop(0, (share // 8) * wide, block, 0)
    scale = math.sqrt(width) * scale_of(rows_ref[...]) * scale_ref[:1, :]
    return best[...] / scale


def first_kernel(rows_ref, turned_ref, order_ref, ends_ref, scale_ref, out_ref, best, pair, terms):
    out_ref[...] = round_scores(
        False, rows_ref, turned_ref, order_ref, ends_ref, scale_ref, best, pair, terms
    )


def last_kernel(before_ref, rows_ref, turned_ref, order_ref, ends_ref, scale_ref, out_ref, best, pair, terms):
    value = round_scores(True, rows_ref, turned_ref, order_ref, ends_ref, scale_ref, best, pair, terms)
    share, images = value.shape
    fill = jnp.zeros((LANES - ROUNDS * share, images), jnp.float32)
    turned = jnp.transpose(jnp.concatenate([before_ref[...], value, fill], axis=0))
    lane = lax.broadcasted_iota(jnp.int32, (share // 2, LANES), 1)
    for g in range(images // share):
        top = turned[g * share : g * share + share // 2]
        low = pltpu.roll(turned[g * share + share // 2 : (g + 1) * share], LANES // 2, 1)
        out_ref[g] = jnp.where(lane < LANES // 2, top, low)


def place_kernel(pieces_ref, out_ref):
    count, short, _ = pieces_ref.shape
    share = 2 * short
    lane = lax.broadcasted_iota(jnp.int32, (short, LANES), 1)
    for r in range(ROUNDS):
        for h in range(2):
            for column in range(count * share // LANES):
                whole = None
                for k in range(LANES // share):
                    shift = (k * share - h * (LANES // 2) - r * share) % LANES
                    piece = pieces_ref[column * (LANES // share) + k]
                    piece = pltpu.roll(piece, shift, 1) if shift else piece
                    whole = piece if whole is None else jnp.where(lane < k * share, whole, piece)
                out_ref[r, h * short : (h + 1) * short, column * LANES : (column + 1) * LANES] = whole


VMEM = pl.BlockSpec(memory_space=pltpu.VMEM)
SMEM = pl.BlockSpec(memory_space=pltpu.SMEM)
HBM = pl.BlockSpec(memory_space=pltpu.HBM)


def call(kernel, inputs, shapes, in_specs=None, out_specs=None, scratch=(), flops=0):
    return pl.pallas_call(
        kernel,
        out_shape=shapes,
        in_specs=in_specs or [VMEM] * len(inputs),
        out_specs=out_specs or jax.tree.map(lambda _: VMEM, shapes),
        scratch_shapes=list(scratch),
        compiler_params=pltpu.CompilerParams(vmem_limit_bytes=32 * 2**20),
        cost_estimate=pl.CostEstimate(flops=flops, bytes_accessed=2**21, transcendentals=0),
    )(*inputs)


def from_chip(index, chips, rows, beside):
    def moved(apart):
        pairs = [(source, source ^ (2 * apart)) for source in range(2 * chips)]

        def branch(piece, *others):
            there = lax.ppermute(piece, "blk", pairs) if apart else piece
            return there, beside(*others)

        return branch

    return lax.switch(index, [moved(apart) for apart in range(chips)], *rows)


def per_device(coeffs, orders, plan):
    ang_count = lax.axis_size("ang")
    blocks = lax.axis_size("blk")
    images, width = coeffs.shape
    half = width // 2
    tiles = half // LANES
    share = images // ang_count
    f32, bf16, i32 = jnp.float32, jnp.bfloat16, jnp.int32
    shape = jax.ShapeDtypeStruct

    first, second, turned, own_rows, order, ends, scale = call(
        prepare_kernel,
        tuple(
            pltpu.with_memory_space_constraint(x, pltpu.HBM) for x in (coeffs, orders.reshape(1, half), plan)
        ),
        (
            shape((1,), i32),
            shape((1,), i32),
            shape((width, images), bf16),
            shape((share, width), bf16),
            shape((1, width), i32),
            shape((2 * tiles,), i32),
            shape((8, images), f32),
        ),
        [HBM, HBM, HBM],
        (SMEM, SMEM, VMEM, VMEM, VMEM, SMEM, VMEM),
        [
            pltpu.VMEM((images, width), bf16),
            pltpu.VMEM((1, half), i32),
            pltpu.SMEM((ROUNDS,), i32),
            pltpu.VMEM((half, half), bf16),
            pltpu.VMEM((images, width), bf16),
            pltpu.SemaphoreType.DMA((3,)),
        ],
        flops=2 * images * width * half,
    )
    other_rows = lax.ppermute(own_rows, "blk", [(source, source ^ 1) for source in range(blocks)])
    sent = call(
        choose_kernel,
        (plan, own_rows, other_rows),
        (shape((share, width), bf16),) * 2,
        [SMEM, VMEM, VMEM],
    )
    rows = 2 * share
    scratch = [
        pltpu.VMEM((share, images), f32),
        pltpu.VMEM((rows, width), bf16),
        pltpu.VMEM(((ORDERS + GROUP) * rows, images), f32),
    ]
    shared = (turned, order, ends, scale)
    flops = 2 * images * width * rows * 8

    def score_first(rows, *shared):
        return call(
            first_kernel,
            (rows, *shared),
            shape((share, images), f32),
            [VMEM, VMEM, VMEM, SMEM, VMEM],
            scratch=scratch,
            flops=flops,
        )

    rows_first, _ = from_chip(first[0], blocks // 2, (sent[0],), lambda: ())
    rows_second, before = from_chip(
        second[0], blocks // 2, (sent[1], rows_first, *shared), score_first
    )
    pieces = call(
        last_kernel,
        (before, rows_second, *shared),
        shape((ang_count, share // 2, LANES), f32),
        [VMEM, VMEM, VMEM, VMEM, SMEM, VMEM],
        scratch=scratch,
        flops=flops,
    )
    pieces = lax.all_to_all(pieces, "ang", 0, 0, tiled=True)
    return call(place_kernel, (pieces,), shape((ROUNDS, share, images), f32))


def solution(mesh):
    in_specs = (P("blk", None), P(), P())
    out_specs = P(None, ("blk", "ang"), None)
    return jax.shard_map(
        per_device, mesh=mesh, in_specs=in_specs, out_specs=out_specs, check_vma=False
    )
```

```python
import functools
import math

import jax
import jax.numpy as jnp
from jax import lax
from jax.experimental import pallas as pl
from jax.experimental.pallas import tpu as pltpu
from jax.sharding import PartitionSpec as P

ANGLES = 128
ORDERS = 48
ROUNDS = 2
LANES = 128
GROUP = 8
CHAINS = 4


def plus(u, v):
    if u is None or v is None:
        return u if v is None else v
    (su, a), (sv, b) = u, v
    if su == sv:
        return (su, a + b)
    return (1, a - b) if su > 0 else (1, b - a)


def negative(u):
    return None if u is None else (-u[0], u[1])


def minus(u, v):
    return plus(u, negative(v))


def times(u, factor):
    return None if u is None else (u[0], u[1] * jnp.float32(factor))


def plain(u):
    return u[1] if u[0] > 0 else -u[1]


def cosine_sums(x):
    size = len(x)
    if size == 1:
        return [x[0]]
    half = size // 2
    even = cosine_sums([plus(x[n], x[size - 1 - n]) for n in range(half)])
    odd = cosine_sums(
        [
            times(minus(x[n], x[size - 1 - n]), 2.0 * math.cos(math.pi * (2 * n + 1) / (2 * size)))
            for n in range(half)
        ]
    )
    out = [None] * size
    for a in range(half):
        out[2 * a] = even[a]
        out[2 * a + 1] = times(odd[0], 0.5) if a == 0 else minus(odd[a], out[2 * a - 1])
    return out


def padded(x, size):
    return x + [None] * (size - len(x))


def cosine_series(terms, period):
    if len(terms) == 1:
        return [terms[0]] * (period // 2 + 1)
    quarter = period // 4
    even = cosine_series(terms[0::2], period // 2)
    odd = cosine_sums(padded(terms[1::2], quarter)) + [None]
    out = [None] * (period // 2 + 1)
    for a in range(quarter + 1):
        out[a] = plus(even[a], odd[a])
        out[period // 2 - a] = minus(even[a], odd[a])
    return out


def sine_series(terms, period):
    if len(terms) == 1:
        return [None] * (period // 2 + 1)
    quarter = period // 4
    even = sine_series(terms[0::2], period // 2)
    flipped = [u if n % 2 == 0 else negative(u) for n, u in enumerate(terms[1::2])]
    odd = [None] + cosine_sums(padded(flipped, quarter))[::-1]
    out = [None] * (period // 2 + 1)
    for a in range(quarter + 1):
        out[period // 2 - a] = minus(odd[a], even[a])
        out[a] = plus(even[a], odd[a])
    return out


def best_angle(cosine_terms, sine_terms):
    across = cosine_series([(1, u) for u in cosine_terms], ANGLES)
    along = sine_series([(1, u) for u in sine_terms], ANGLES)
    best = [None] * CHAINS
    for n, (u, v) in enumerate(zip(across, along, strict=True)):
        value = plain(u)
        if v is not None:
            value = value + jnp.abs(v[1])
        k = n % CHAINS
        best[k] = value if best[k] is None else jnp.maximum(best[k], value)
    return functools.reduce(jnp.maximum, best)


def scale_of(rows):
    wide = rows.astype(jnp.float32)
    return jnp.sqrt(jnp.mean(wide * wide, axis=1, keepdims=True) + 1e-06)


def prepare_kernel(
    own_hbm, orders_hbm, plan_hbm, first_ref, second_ref, turned_ref, rows_ref, order_ref, ends_ref, scale_ref,
    own, orders, plan, select, gathered, arrived
):
    half = orders.shape[1]
    images = own.shape[0]
    share = rows_ref.shape[0]
    tiles = half // LANES
    copies = [
        pltpu.make_async_copy(source, target, arrived.at[n])
        for n, (source, target) in enumerate(((orders_hbm, orders), (plan_hbm, plan), (own_hbm, own)))
    ]
    for copy in copies:
        copy.start()
    copies[0].wait()
    keys = orders[...] * half + lax.broadcasted_iota(jnp.int32, (1, half), 1)
    keys = keys.astype(jnp.float32)
    keys_down = jnp.transpose(jnp.broadcast_to(keys, (LANES, half)))
    place = jnp.zeros((1, half), jnp.float32)
    for c in range(tiles):
        behind = keys_down[c * LANES : (c + 1) * LANES, :1] < keys
        place = place + jnp.sum(jnp.where(behind, 1.0, 0.0), axis=0, keepdims=True)
    place = jnp.transpose(jnp.broadcast_to(place, (LANES, half))).astype(jnp.int32)
    spot = lax.broadcasted_iota(jnp.int32, (LANES, half), 1)
    for c in range(tiles):
        rows = slice(c * LANES, (c + 1) * LANES)
        select[rows, :] = jnp.where(spot == place[rows, :1], 1.0, 0.0).astype(jnp.bfloat16)
    wide = jnp.broadcast_to(orders[...].astype(jnp.float32), (16, half)).astype(jnp.bfloat16)
    order = jnp.dot(wide, select[...], preferred_element_type=jnp.float32)[:1].astype(jnp.int32)
    for t in range(tiles):
        part = order[:, t * LANES : (t + 1) * LANES]
        order_ref[:, 2 * t * LANES : (2 * t + 1) * LANES] = part
        order_ref[:, (2 * t + 1) * LANES : (2 * t + 2) * LANES] = part
        ends_ref[2 * t] = jnp.min(part)
        ends_ref[2 * t + 1] = jnp.max(part)
    copies[1].wait()
    first_ref[0] = lax.shift_right_logical(plan[0], 1)
    second_ref[0] = lax.shift_right_logical(plan[1], 1)
    copies[2].wait()
    for side in range(2):
        moved = jnp.dot(
            own[:, side * half : (side + 1) * half], select[...], preferred_element_type=jnp.float32
        ).astype(jnp.bfloat16)
        for t in range(tiles):
            there = slice((2 * t + side) * LANES, (2 * t + side + 1) * LANES)
            part = moved[:, t * LANES : (t + 1) * LANES]
            gathered[:, there] = part
            turned_ref[there, :] = jnp.transpose(part)
    mine = pl.ds(pl.multiple_of(lax.axis_index("ang") * share, share), share)
    rows_ref[...] = gathered[mine, :]
    scale_ref[...] = jnp.transpose(jnp.broadcast_to(scale_of(own[...]), (images, LANES)))[:8]


def choose_kernel(plan_ref, own_ref, other_ref, first_ref, second_ref):
    for r, ref in enumerate((first_ref, second_ref)):
        crossed = (plan_ref[r] & 1) == 1

        @pl.when(crossed)
        def _(ref=ref):
            ref[...] = other_ref[...]

        @pl.when(jnp.logical_not(crossed))
        def _(ref=ref):
            ref[...] = own_ref[...]


def add_tile(cols, base, order_ref, turned_ref, pair, terms):
    rows = pair.shape[0]
    here, block = order_ref[:, cols], pair[:, cols]
    masked = jnp.concatenate(
        [block * jnp.where(here == base + q, 1.0, 0.0).astype(jnp.bfloat16) for q in range(GROUP)], axis=0
    )
    found = jnp.dot(masked, turned_ref[cols, :], preferred_element_type=jnp.float32)
    terms[pl.ds(pl.multiple_of(base * rows, rows), GROUP * rows), :] += found


def round_scores(straight, rows_ref, turned_ref, order_ref, ends_ref, scale_ref, best, pair, terms):
    share, width = rows_ref.shape
    images = turned_ref.shape[1]
    tiles = width // (2 * LANES)
    rows = 2 * share
    cleared = GROUP * rows

    def clear(n, _):
        at = pl.ds(pl.multiple_of(n * cleared, cleared), cleared)
        terms[at, :] = jnp.zeros((cleared, images), jnp.float32)
        return 0

    def couple(t, _):
        one = pl.ds(pl.multiple_of(2 * t * LANES, LANES), LANES)
        two = pl.ds(pl.multiple_of((2 * t + 1) * LANES, LANES), LANES)
        x, y = rows_ref[:, one], rows_ref[:, two]
        pair[:share, one] = x
        pair[:share, two] = y
        pair[share:, one] = y
        pair[share:, two] = -x
        return 0

    lax.fori_loop(0, (ORDERS + GROUP) // GROUP, clear, 0)
    lax.fori_loop(0, tiles, couple, 0)
    if straight:
        for t in range(tiles):
            cols = slice(2 * t * LANES, (2 * t + 2) * LANES)
            add_tile(cols, ends_ref[2 * t], order_ref, turned_ref, pair, terms)

    def tile(t, _):
        least, most = ends_ref[2 * t], ends_ref[2 * t + 1]
        cols = pl.ds(pl.multiple_of(2 * t * LANES, 2 * LANES), 2 * LANES)

        def step(c, _):
            add_tile(cols, least + GROUP * c, order_ref, turned_ref, pair, terms)
            return 0

        return lax.fori_loop(1 if straight else 0, (most - least) // GROUP + 1, step, 0)

    lax.fori_loop(0, tiles, tile, 0)
    across = images if straight else LANES
    count = images // across

    def block(n, _):
        lane = pl.ds(pl.multiple_of(lax.rem(n, count) * across, LANES), across)
        j = pl.multiple_of(n // count * 8, 8)
        cosine_terms = [terms[pl.ds(m * rows + j, 8), lane] for m in range(ORDERS)]
        sine_terms = [terms[pl.ds(m * rows + share + j, 8), lane] for m in range(ORDERS)]
        best[pl.ds(j, 8), lane] = best_angle(cosine_terms, sine_terms)
        return 0

    lax.fori_loop(0, (share // 8) * count, block, 0)
    scale = math.sqrt(width) * scale_of(rows_ref[...]) * scale_ref[:1, :]
    return best[...] / scale


def first_kernel(rows_ref, turned_ref, order_ref, ends_ref, scale_ref, out_ref, best, pair, terms):
    out_ref[...] = round_scores(
        False, rows_ref, turned_ref, order_ref, ends_ref, scale_ref, best, pair, terms
    )


def last_kernel(before_ref, rows_ref, turned_ref, order_ref, ends_ref, scale_ref, out_ref, best, pair, terms):
    value = round_scores(True, rows_ref, turned_ref, order_ref, ends_ref, scale_ref, best, pair, terms)
    share, images = value.shape
    fill = jnp.zeros((LANES - ROUNDS * share, images), jnp.float32)
    turned = jnp.transpose(jnp.concatenate([before_ref[...], value, fill], axis=0))
    lane = lax.broadcasted_iota(jnp.int32, (share // 2, LANES), 1)
    for g in range(images // share):
        top = turned[g * share : g * share + share // 2]
        low = pltpu.roll(turned[g * share + share // 2 : (g + 1) * share], LANES // 2, 1)
        out_ref[g] = jnp.where(lane < LANES // 2, top, low)


def place_kernel(pieces_ref, out_ref):
    count, short, _ = pieces_ref.shape
    share = 2 * short
    lane = lax.broadcasted_iota(jnp.int32, (short, LANES), 1)
    for r in range(ROUNDS):
        for h in range(2):
            for column in range(count * share // LANES):
                whole = None
                for k in range(LANES // share):
                    shift = (k * share - h * (LANES // 2) - r * share) % LANES
                    piece = pieces_ref[column * (LANES // share) + k]
                    piece = pltpu.roll(piece, shift, 1) if shift else piece
                    whole = piece if whole is None else jnp.where(lane < k * share, whole, piece)
                out_ref[r, h * short : (h + 1) * short, column * LANES : (column + 1) * LANES] = whole


VMEM = pl.BlockSpec(memory_space=pltpu.VMEM)
SMEM = pl.BlockSpec(memory_space=pltpu.SMEM)
HBM = pl.BlockSpec(memory_space=pltpu.HBM)


def call(kernel, inputs, shapes, in_specs=None, out_specs=None, scratch=(), flops=0):
    return pl.pallas_call(
        kernel,
        out_shape=shapes,
        in_specs=in_specs or [VMEM] * len(inputs),
        out_specs=out_specs or jax.tree.map(lambda _: VMEM, shapes),
        scratch_shapes=list(scratch),
        compiler_params=pltpu.CompilerParams(vmem_limit_bytes=32 * 2**20),
        cost_estimate=pl.CostEstimate(flops=flops, bytes_accessed=2**21, transcendentals=0),
    )(*inputs)


def from_chip(index, chips, rows, beside):
    def moved(apart):
        pairs = [(source, source ^ (2 * apart)) for source in range(2 * chips)]

        def branch(piece, *others):
            there = lax.ppermute(piece, "blk", pairs) if apart else piece
            return there, beside(*others)

        return branch

    return lax.switch(index, [moved(apart) for apart in range(chips)], *rows)


def per_device(coeffs, orders, plan):
    ang_count = lax.axis_size("ang")
    blocks = lax.axis_size("blk")
    images, width = coeffs.shape
    half = width // 2
    tiles = half // LANES
    share = images // ang_count
    f32, bf16, i32 = jnp.float32, jnp.bfloat16, jnp.int32
    shape = jax.ShapeDtypeStruct

    first, second, turned, own_rows, order, ends, scale = call(
        prepare_kernel,
        tuple(
            pltpu.with_memory_space_constraint(x, pltpu.HBM) for x in (coeffs, orders.reshape(1, half), plan)
        ),
        (
            shape((1,), i32),
            shape((1,), i32),
            shape((width, images), bf16),
            shape((share, width), bf16),
            shape((1, width), i32),
            shape((2 * tiles,), i32),
            shape((8, images), f32),
        ),
        [HBM, HBM, HBM],
        (SMEM, SMEM, VMEM, VMEM, VMEM, SMEM, VMEM),
        [
            pltpu.VMEM((images, width), bf16),
            pltpu.VMEM((1, half), i32),
            pltpu.SMEM((ROUNDS,), i32),
            pltpu.VMEM((half, half), bf16),
            pltpu.VMEM((images, width), bf16),
            pltpu.SemaphoreType.DMA((3,)),
        ],
        flops=2 * images * width * half,
    )
    other_rows = lax.ppermute(own_rows, "blk", [(source, source ^ 1) for source in range(blocks)])
    sent = call(
        choose_kernel,
        (plan, own_rows, other_rows),
        (shape((share, width), bf16),) * 2,
        [SMEM, VMEM, VMEM],
    )
    rows = 2 * share
    scratch = [
        pltpu.VMEM((share, images), f32),
        pltpu.VMEM((rows, width), bf16),
        pltpu.VMEM(((ORDERS + GROUP) * rows, images), f32),
    ]
    shared = (turned, order, ends, scale)
    flops = 2 * images * width * rows * 8

    def score_first(rows, *shared):
        return call(
            first_kernel,
            (rows, *shared),
            shape((share, images), f32),
            [VMEM, VMEM, VMEM, SMEM, VMEM],
            scratch=scratch,
            flops=flops,
        )

    rows_first, _ = from_chip(first[0], blocks // 2, (sent[0],), lambda: ())
    rows_second, before = from_chip(
        second[0], blocks // 2, (sent[1], rows_first, *shared), score_first
    )
    pieces = call(
        last_kernel,
        (before, rows_second, *shared),
        shape((ang_count, share // 2, LANES), f32),
        [VMEM, VMEM, VMEM, VMEM, SMEM, VMEM],
        scratch=scratch,
        flops=flops,
    )
    pieces = lax.all_to_all(pieces, "ang", 0, 0, tiled=True)
    return call(place_kernel, (pieces,), shape((ROUNDS, share, images), f32))


def solution(mesh):
    in_specs = (P("blk", None), P(), P())
    out_specs = P(None, ("blk", "ang"), None)
    return jax.shard_map(
        per_device, mesh=mesh, in_specs=in_specs, out_specs=out_specs, check_vma=False
    )
```

```python
import functools
import math

import jax
import jax.numpy as jnp
from jax import lax
from jax.experimental import pallas as pl
from jax.experimental.pallas import tpu as pltpu
from jax.sharding import PartitionSpec as P

ANGLES = 128
ORDERS = 48
ROUNDS = 2
LANES = 128
GROUP = 8
CHAINS = 4
KINDS = 64


def plus(u, v):
    if u is None or v is None:
        return u if v is None else v
    (su, a), (sv, b) = u, v
    if su == sv:
        return (su, a + b)
    return (1, a - b) if su > 0 else (1, b - a)


def negative(u):
    return None if u is None else (-u[0], u[1])


def minus(u, v):
    return plus(u, negative(v))


def times(u, factor):
    return None if u is None else (u[0], u[1] * jnp.float32(factor))


def plain(u):
    return u[1] if u[0] > 0 else -u[1]


def cosine_sums(x):
    size = len(x)
    if size == 1:
        return [x[0]]
    half = size // 2
    even = cosine_sums([plus(x[n], x[size - 1 - n]) for n in range(half)])
    odd = cosine_sums(
        [
            times(minus(x[n], x[size - 1 - n]), 2.0 * math.cos(math.pi * (2 * n + 1) / (2 * size)))
            for n in range(half)
        ]
    )
    out = [None] * size
    for a in range(half):
        out[2 * a] = even[a]
        out[2 * a + 1] = times(odd[0], 0.5) if a == 0 else minus(odd[a], out[2 * a - 1])
    return out


def padded(x, size):
    return x + [None] * (size - len(x))


def cosine_series(terms, period):
    if len(terms) == 1:
        return [terms[0]] * (period // 2 + 1)
    quarter = period // 4
    even = cosine_series(terms[0::2], period // 2)
    odd = cosine_sums(padded(terms[1::2], quarter)) + [None]
    out = [None] * (period // 2 + 1)
    for a in range(quarter + 1):
        out[a] = plus(even[a], odd[a])
        out[period // 2 - a] = minus(even[a], odd[a])
    return out


def sine_series(terms, period):
    if len(terms) == 1:
        return [None] * (period // 2 + 1)
    quarter = period // 4
    even = sine_series(terms[0::2], period // 2)
    flipped = [u if n % 2 == 0 else negative(u) for n, u in enumerate(terms[1::2])]
    odd = [None] + cosine_sums(padded(flipped, quarter))[::-1]
    out = [None] * (period // 2 + 1)
    for a in range(quarter + 1):
        out[period // 2 - a] = minus(odd[a], even[a])
        out[a] = plus(even[a], odd[a])
    return out


def best_angle(cosine_terms, sine_terms):
    across = cosine_series([(1, u) for u in cosine_terms], ANGLES)
    along = sine_series([(1, u) for u in sine_terms], ANGLES)
    best = [None] * CHAINS
    for n, (u, v) in enumerate(zip(across, along, strict=True)):
        value = plain(u)
        if v is not None:
            value = value + jnp.abs(v[1])
        k = n % CHAINS
        best[k] = value if best[k] is None else jnp.maximum(best[k], value)
    return functools.reduce(jnp.maximum, best)


def scale_of(rows):
    wide = rows.astype(jnp.float32)
    return jnp.sqrt(jnp.mean(wide * wide, axis=1, keepdims=True) + 1e-06)


def prepare_kernel(
    own_hbm, orders_hbm, plan_hbm, first_ref, second_ref, crossed_ref, turned_ref, rows_ref, order_ref, ends_ref, scale_ref,
    own, orders, plan, select, gathered, arrived
):
    half = orders.shape[1]
    images = own.shape[0]
    share = rows_ref.shape[0]
    tiles = half // LANES
    copies = [
        pltpu.make_async_copy(source, target, arrived.at[n])
        for n, (source, target) in enumerate(((orders_hbm, orders), (plan_hbm, plan), (own_hbm, own)))
    ]
    for copy in copies:
        copy.start()
    copies[0].wait()
    row = lax.broadcasted_iota(jnp.int32, (LANES, 2 * LANES), 0)
    column = lax.broadcasted_iota(jnp.int32, (LANES, 2 * LANES), 1)
    earlier = jnp.where((row < column) | (column >= LANES), 1.0, 0.0).astype(jnp.bfloat16)
    which = lax.broadcasted_iota(jnp.int32, (KINDS, half), 0)
    count = jnp.sum(jnp.where(orders[...] < which, 1.0, 0.0), axis=1, keepdims=True)
    count = jnp.broadcast_to(count, (KINDS, LANES))
    same = jnp.where(orders[...] == which, 1.0, 0.0)
    places = []
    for c in range(tiles):
        part = same[:, c * LANES : (c + 1) * LANES]
        found = jnp.dot(part.astype(jnp.bfloat16), earlier, preferred_element_type=jnp.float32)
        places.append(jnp.sum(part * (count + found[:, :LANES]), axis=0, keepdims=True))
        count = count + found[:, LANES:]
    place = jnp.concatenate(places, axis=1)
    place = jnp.transpose(jnp.broadcast_to(place, (LANES, half))).astype(jnp.int32)
    spot = lax.broadcasted_iota(jnp.int32, (LANES, half), 1)
    for c in range(tiles):
        rows = slice(c * LANES, (c + 1) * LANES)
        select[rows, :] = jnp.where(spot == place[rows, :1], 1.0, 0.0).astype(jnp.bfloat16)
    wide = jnp.broadcast_to(orders[...].astype(jnp.float32), (16, half)).astype(jnp.bfloat16)
    order = jnp.dot(wide, select[...], preferred_element_type=jnp.float32)[:1].astype(jnp.int32)
    for t in range(tiles):
        part = order[:, t * LANES : (t + 1) * LANES]
        order_ref[:, 2 * t * LANES : (2 * t + 1) * LANES] = part
        order_ref[:, (2 * t + 1) * LANES : (2 * t + 2) * LANES] = part
        ends_ref[2 * t] = jnp.min(part)
        ends_ref[2 * t + 1] = jnp.max(part)
    copies[1].wait()
    first_ref[0] = lax.shift_right_logical(plan[0], 1)
    second_ref[0] = lax.shift_right_logical(plan[1], 1)
    for r in range(ROUNDS):
        crossed_ref[r : r + 1, :] = jnp.full((1, 2 * half), plan[r] & 1, jnp.int32)
    copies[2].wait()
    for side in range(2):
        moved = jnp.dot(
            own[:, side * half : (side + 1) * half], select[...], preferred_element_type=jnp.float32
        ).astype(jnp.bfloat16)
        for t in range(tiles):
            there = slice((2 * t + side) * LANES, (2 * t + side + 1) * LANES)
            part = moved[:, t * LANES : (t + 1) * LANES]
            gathered[:, there] = part
            turned_ref[there, :] = jnp.transpose(part)
    mine = pl.ds(pl.multiple_of(lax.axis_index("ang") * share, share), share)
    rows_ref[...] = gathered[mine, :]
    scale_ref[...] = jnp.transpose(jnp.broadcast_to(scale_of(own[...]), (images, LANES)))[:8]


def add_tile(cols, base, order_ref, turned_ref, pair, terms):
    rows = pair.shape[0]
    here, block = order_ref[:, cols], pair[:, cols]
    masked = jnp.concatenate(
        [block * jnp.where(here == base + q, 1.0, 0.0).astype(jnp.bfloat16) for q in range(GROUP)], axis=0
    )
    found = jnp.dot(masked, turned_ref[cols, :], preferred_element_type=jnp.float32)
    terms[pl.ds(pl.multiple_of(base * rows, rows), GROUP * rows), :] += found


def round_scores(straight, rows_ref, turned_ref, order_ref, ends_ref, scale_ref, best, pair, terms):
    share, width = rows_ref.shape
    images = turned_ref.shape[1]
    tiles = width // (2 * LANES)
    rows = 2 * share
    cleared = GROUP * rows

    def clear(n, _):
        at = pl.ds(pl.multiple_of(n * cleared, cleared), cleared)
        terms[at, :] = jnp.zeros((cleared, images), jnp.float32)
        return 0

    def couple(t, _):
        one = pl.ds(pl.multiple_of(2 * t * LANES, LANES), LANES)
        two = pl.ds(pl.multiple_of((2 * t + 1) * LANES, LANES), LANES)
        x, y = rows_ref[:, one], rows_ref[:, two]
        pair[:share, one] = x
        pair[:share, two] = y
        pair[share:, one] = y
        pair[share:, two] = -x
        return 0

    lax.fori_loop(0, (ORDERS + GROUP) // GROUP, clear, 0)
    lax.fori_loop(0, tiles, couple, 0)
    if straight:
        for t in range(tiles):
            cols = slice(2 * t * LANES, (2 * t + 2) * LANES)
            add_tile(cols, ends_ref[2 * t], order_ref, turned_ref, pair, terms)

    def tile(t, _):
        least, most = ends_ref[2 * t], ends_ref[2 * t + 1]
        cols = pl.ds(pl.multiple_of(2 * t * LANES, 2 * LANES), 2 * LANES)

        def step(c, _):
            add_tile(cols, least + GROUP * c, order_ref, turned_ref, pair, terms)
            return 0

        return lax.fori_loop(1 if straight else 0, (most - least) // GROUP + 1, step, 0)

    lax.fori_loop(0, tiles, tile, 0)
    across = images if straight else LANES
    count = images // across

    def block(n, _):
        lane = pl.ds(pl.multiple_of(lax.rem(n, count) * across, LANES), across)
        j = pl.multiple_of(n // count * 8, 8)
        cosine_terms = [terms[pl.ds(m * rows + j, 8), lane] for m in range(ORDERS)]
        sine_terms = [terms[pl.ds(m * rows + share + j, 8), lane] for m in range(ORDERS)]
        best[pl.ds(j, 8), lane] = best_angle(cosine_terms, sine_terms)
        return 0

    lax.fori_loop(0, (share // 8) * count, block, 0)
    scale = math.sqrt(width) * scale_of(rows_ref[...]) * scale_ref[:1, :]
    return best[...] / scale


def first_kernel(rows_ref, turned_ref, order_ref, ends_ref, scale_ref, out_ref, best, pair, terms):
    out_ref[...] = round_scores(
        False, rows_ref, turned_ref, order_ref, ends_ref, scale_ref, best, pair, terms
    )


def last_kernel(before_ref, rows_ref, turned_ref, order_ref, ends_ref, scale_ref, out_ref, best, pair, terms):
    value = round_scores(True, rows_ref, turned_ref, order_ref, ends_ref, scale_ref, best, pair, terms)
    share, images = value.shape
    fill = jnp.zeros((LANES - ROUNDS * share, images), jnp.float32)
    turned = jnp.transpose(jnp.concatenate([before_ref[...], value, fill], axis=0))
    lane = lax.broadcasted_iota(jnp.int32, (share // 2, LANES), 1)
    for g in range(images // share):
        top = turned[g * share : g * share + share // 2]
        low = pltpu.roll(turned[g * share + share // 2 : (g + 1) * share], LANES // 2, 1)
        out_ref[g] = jnp.where(lane < LANES // 2, top, low)


def place_kernel(pieces_ref, out_ref):
    count, short, _ = pieces_ref.shape
    share = 2 * short
    lane = lax.broadcasted_iota(jnp.int32, (short, LANES), 1)
    for r in range(ROUNDS):
        for h in range(2):
            for column in range(count * share // LANES):
                whole = None
                for k in range(LANES // share):
                    shift = (k * share - h * (LANES // 2) - r * share) % LANES
                    piece = pieces_ref[column * (LANES // share) + k]
                    piece = pltpu.roll(piece, shift, 1) if shift else piece
                    whole = piece if whole is None else jnp.where(lane < k * share, whole, piece)
                out_ref[r, h * short : (h + 1) * short, column * LANES : (column + 1) * LANES] = whole


VMEM = pl.BlockSpec(memory_space=pltpu.VMEM)
SMEM = pl.BlockSpec(memory_space=pltpu.SMEM)
HBM = pl.BlockSpec(memory_space=pltpu.HBM)


def call(kernel, inputs, shapes, in_specs=None, out_specs=None, scratch=(), flops=0):
    return pl.pallas_call(
        kernel,
        out_shape=shapes,
        in_specs=in_specs or [VMEM] * len(inputs),
        out_specs=out_specs or jax.tree.map(lambda _: VMEM, shapes),
        scratch_shapes=list(scratch),
        compiler_params=pltpu.CompilerParams(vmem_limit_bytes=32 * 2**20),
        cost_estimate=pl.CostEstimate(flops=flops, bytes_accessed=2**21, transcendentals=0),
    )(*inputs)


def from_chip(index, chips, rows, beside):
    def moved(apart):
        pairs = [(source, source ^ (2 * apart)) for source in range(2 * chips)]

        def branch(piece, *others):
            there = lax.ppermute(piece, "blk", pairs) if apart else piece
            return there, beside(*others)

        return branch

    return lax.switch(index, [moved(apart) for apart in range(chips)], *rows)


def per_device(coeffs, orders, plan):
    ang_count = lax.axis_size("ang")
    blocks = lax.axis_size("blk")
    images, width = coeffs.shape
    half = width // 2
    tiles = half // LANES
    share = images // ang_count
    f32, bf16, i32 = jnp.float32, jnp.bfloat16, jnp.int32
    shape = jax.ShapeDtypeStruct

    first, second, crossed, turned, own_rows, order, ends, scale = call(
        prepare_kernel,
        tuple(
            pltpu.with_memory_space_constraint(x, pltpu.HBM) for x in (coeffs, orders.reshape(1, half), plan)
        ),
        (
            shape((1,), i32),
            shape((1,), i32),
            shape((ROUNDS, width), i32),
            shape((width, images), bf16),
            shape((share, width), bf16),
            shape((1, width), i32),
            shape((2 * tiles,), i32),
            shape((8, images), f32),
        ),
        [HBM, HBM, HBM],
        (SMEM, SMEM, VMEM, VMEM, VMEM, VMEM, SMEM, VMEM),
        [
            pltpu.VMEM((images, width), bf16),
            pltpu.VMEM((1, half), i32),
            pltpu.SMEM((ROUNDS,), i32),
            pltpu.VMEM((half, half), bf16),
            pltpu.VMEM((images, width), bf16),
            pltpu.SemaphoreType.DMA((3,)),
        ],
        flops=2 * images * width * half,
    )
    other_rows = lax.ppermute(own_rows, "blk", [(source, source ^ 1) for source in range(blocks)])
    sent = [jnp.where(crossed[r][None, :] != 0, other_rows, own_rows) for r in range(ROUNDS)]
    rows = 2 * share
    scratch = [
        pltpu.VMEM((share, images), f32),
        pltpu.VMEM((rows, width), bf16),
        pltpu.VMEM(((ORDERS + GROUP) * rows, images), f32),
    ]
    shared = (turned, order, ends, scale)
    flops = 2 * images * width * rows * 8

    def score_first(rows, *shared):
        return call(
            first_kernel,
            (rows, *shared),
            shape((share, images), f32),
            [VMEM, VMEM, VMEM, SMEM, VMEM],
            scratch=scratch,
            flops=flops,
        )

    rows_first, _ = from_chip(first[0], blocks // 2, (sent[0],), lambda: ())
    rows_second, before = from_chip(
        second[0], blocks // 2, (sent[1], rows_first, *shared), score_first
    )
    pieces = call(
        last_kernel,
        (before, rows_second, *shared),
        shape((ang_count, share // 2, LANES), f32),
        [VMEM, VMEM, VMEM, VMEM, SMEM, VMEM],
        scratch=scratch,
        flops=flops,
    )
    pieces = lax.all_to_all(pieces, "ang", 0, 0, tiled=True)
    return call(place_kernel, (pieces,), shape((ROUNDS, share, images), f32))


def solution(mesh):
    in_specs = (P("blk", None), P(), P())
    out_specs = P(None, ("blk", "ang"), None)
    return jax.shard_map(
        per_device, mesh=mesh, in_specs=in_specs, out_specs=out_specs, check_vma=False
    )
```

```python
import functools
import math

import jax
import jax.numpy as jnp
from jax import lax
from jax.experimental import pallas as pl
from jax.experimental.pallas import tpu as pltpu
from jax.sharding import PartitionSpec as P

ANGLES = 128
ORDERS = 48
ROUNDS = 2
LANES = 128
GROUP = 8
CHAINS = 4
KINDS = 64


def plus(u, v):
    if u is None or v is None:
        return u if v is None else v
    (su, a), (sv, b) = u, v
    if su == sv:
        return (su, a + b)
    return (1, a - b) if su > 0 else (1, b - a)


def negative(u):
    return None if u is None else (-u[0], u[1])


def minus(u, v):
    return plus(u, negative(v))


def times(u, factor):
    return None if u is None else (u[0], u[1] * jnp.float32(factor))


def plain(u):
    return u[1] if u[0] > 0 else -u[1]


def cosine_sums(x):
    size = len(x)
    if size == 1:
        return [x[0]]
    half = size // 2
    even = cosine_sums([plus(x[n], x[size - 1 - n]) for n in range(half)])
    odd = cosine_sums(
        [
            times(minus(x[n], x[size - 1 - n]), 2.0 * math.cos(math.pi * (2 * n + 1) / (2 * size)))
            for n in range(half)
        ]
    )
    out = [None] * size
    for a in range(half):
        out[2 * a] = even[a]
        out[2 * a + 1] = times(odd[0], 0.5) if a == 0 else minus(odd[a], out[2 * a - 1])
    return out


def padded(x, size):
    return x + [None] * (size - len(x))


def cosine_series(terms, period):
    if len(terms) == 1:
        return [terms[0]] * (period // 2 + 1)
    quarter = period // 4
    even = cosine_series(terms[0::2], period // 2)
    odd = cosine_sums(padded(terms[1::2], quarter)) + [None]
    out = [None] * (period // 2 + 1)
    for a in range(quarter + 1):
        out[a] = plus(even[a], odd[a])
        out[period // 2 - a] = minus(even[a], odd[a])
    return out


def sine_series(terms, period):
    if len(terms) == 1:
        return [None] * (period // 2 + 1)
    quarter = period // 4
    even = sine_series(terms[0::2], period // 2)
    flipped = [u if n % 2 == 0 else negative(u) for n, u in enumerate(terms[1::2])]
    odd = [None] + cosine_sums(padded(flipped, quarter))[::-1]
    out = [None] * (period // 2 + 1)
    for a in range(quarter + 1):
        out[period // 2 - a] = minus(odd[a], even[a])
        out[a] = plus(even[a], odd[a])
    return out


def best_angle(cosine_terms, sine_terms):
    across = cosine_series([(1, u) for u in cosine_terms], ANGLES)
    along = sine_series([(1, u) for u in sine_terms], ANGLES)
    best = [None] * CHAINS
    for n, (u, v) in enumerate(zip(across, along, strict=True)):
        value = plain(u)
        if v is not None:
            value = value + jnp.abs(v[1])
        k = n % CHAINS
        best[k] = value if best[k] is None else jnp.maximum(best[k], value)
    return functools.reduce(jnp.maximum, best)


def scale_of(rows):
    wide = rows.astype(jnp.float32)
    return jnp.sqrt(jnp.mean(wide * wide, axis=1, keepdims=True) + 1e-06)


def reach_of(offset):
    chip = lax.shift_right_logical(offset, 1)
    return jnp.where(chip == 0, 0, jnp.where((chip & 6) == 0, 1, 2))


def prepare_kernel(
    own_hbm, orders_hbm, plan_hbm, first_ref, second_ref, crossed_ref, turned_ref, rows_ref, order_ref, ends_ref, scale_ref,
    own, orders, plan, select, gathered, arrived
):
    half = orders.shape[1]
    images = own.shape[0]
    share = rows_ref.shape[0]
    tiles = half // LANES
    copies = [
        pltpu.make_async_copy(source, target, arrived.at[n])
        for n, (source, target) in enumerate(((orders_hbm, orders), (plan_hbm, plan), (own_hbm, own)))
    ]
    for copy in copies:
        copy.start()
    copies[0].wait()
    row = lax.broadcasted_iota(jnp.int32, (LANES, 2 * LANES), 0)
    column = lax.broadcasted_iota(jnp.int32, (LANES, 2 * LANES), 1)
    earlier = jnp.where((row < column) | (column >= LANES), 1.0, 0.0).astype(jnp.bfloat16)
    which = lax.broadcasted_iota(jnp.int32, (KINDS, half), 0)
    count = jnp.sum(jnp.where(orders[...] < which, 1.0, 0.0), axis=1, keepdims=True)
    spot = lax.broadcasted_iota(jnp.int32, (KINDS, half), 1).astype(jnp.float32)
    begun = jnp.where((count <= spot) & (which > 0), 1.0, 0.0)
    order = jnp.sum(begun, axis=0, keepdims=True).astype(jnp.int32)
    count = jnp.broadcast_to(count, (KINDS, LANES))
    same = jnp.where(orders[...] == which, 1.0, 0.0)
    places = []
    for c in range(tiles):
        part = same[:, c * LANES : (c + 1) * LANES]
        found = jnp.dot(part.astype(jnp.bfloat16), earlier, preferred_element_type=jnp.float32)
        places.append(jnp.sum(part * (count + found[:, :LANES]), axis=0, keepdims=True))
        count = count + found[:, LANES:]
    place = jnp.concatenate(places, axis=1)
    place = jnp.transpose(jnp.broadcast_to(place, (LANES, half))).astype(jnp.int32)
    spot = lax.broadcasted_iota(jnp.int32, (LANES, half), 1)
    for c in range(tiles):
        rows = slice(c * LANES, (c + 1) * LANES)
        select[rows, :] = jnp.where(spot == place[rows, :1], 1.0, 0.0).astype(jnp.bfloat16)
    for t in range(tiles):
        part = order[:, t * LANES : (t + 1) * LANES]
        order_ref[:, 2 * t * LANES : (2 * t + 1) * LANES] = part
        order_ref[:, (2 * t + 1) * LANES : (2 * t + 2) * LANES] = part
        ends_ref[2 * t] = jnp.min(part)
        ends_ref[2 * t + 1] = jnp.max(part)
    copies[1].wait()
    later = (reach_of(plan[0]) > reach_of(plan[1])).astype(jnp.int32)
    ends_ref[2 * tiles] = later
    for r, ref in enumerate((first_ref, second_ref)):
        offset = jnp.where(later == r, plan[0], plan[1])
        ref[0] = lax.shift_right_logical(offset, 1)
        crossed_ref[r : r + 1, :] = jnp.full((1, 2 * half), offset & 1, jnp.int32)
    copies[2].wait()
    for side in range(2):
        moved = jnp.dot(
            own[:, side * half : (side + 1) * half], select[...], preferred_element_type=jnp.float32
        ).astype(jnp.bfloat16)
        for t in range(tiles):
            there = slice((2 * t + side) * LANES, (2 * t + side + 1) * LANES)
            part = moved[:, t * LANES : (t + 1) * LANES]
            gathered[:, there] = part
            turned_ref[there, :] = jnp.transpose(part)
    mine = pl.ds(pl.multiple_of(lax.axis_index("ang") * share, share), share)
    rows_ref[...] = gathered[mine, :]
    scale_ref[...] = jnp.transpose(jnp.broadcast_to(scale_of(own[...]), (images, LANES)))[:8]


def add_tile(cols, base, order_ref, turned_ref, pair, terms):
    rows = pair.shape[0]
    here, block = order_ref[:, cols], pair[:, cols]
    masked = jnp.concatenate(
        [block * jnp.where(here == base + q, 1.0, 0.0).astype(jnp.bfloat16) for q in range(GROUP)], axis=0
    )
    found = jnp.dot(masked, turned_ref[cols, :], preferred_element_type=jnp.float32)
    terms[pl.ds(pl.multiple_of(base * rows, rows), GROUP * rows), :] += found


def round_scores(straight, rows_ref, turned_ref, order_ref, ends_ref, scale_ref, best, pair, terms):
    share, width = rows_ref.shape
    images = turned_ref.shape[1]
    tiles = width // (2 * LANES)
    rows = 2 * share
    cleared = GROUP * rows

    def clear(n, _):
        at = pl.ds(pl.multiple_of(n * cleared, cleared), cleared)
        terms[at, :] = jnp.zeros((cleared, images), jnp.float32)
        return 0

    def couple(t, _):
        one = pl.ds(pl.multiple_of(2 * t * LANES, LANES), LANES)
        two = pl.ds(pl.multiple_of((2 * t + 1) * LANES, LANES), LANES)
        x, y = rows_ref[:, one], rows_ref[:, two]
        pair[:share, one] = x
        pair[:share, two] = y
        pair[share:, one] = y
        pair[share:, two] = -x
        return 0

    lax.fori_loop(0, (ORDERS + GROUP) // GROUP, clear, 0)
    lax.fori_loop(0, tiles, couple, 0)
    if straight:
        for t in range(tiles):
            cols = slice(2 * t * LANES, (2 * t + 2) * LANES)
            add_tile(cols, ends_ref[2 * t], order_ref, turned_ref, pair, terms)

    def tile(t, _):
        least, most = ends_ref[2 * t], ends_ref[2 * t + 1]
        cols = pl.ds(pl.multiple_of(2 * t * LANES, 2 * LANES), 2 * LANES)

        def step(c, _):
            add_tile(cols, least + GROUP * c, order_ref, turned_ref, pair, terms)
            return 0

        return lax.fori_loop(1 if straight else 0, (most - least) // GROUP + 1, step, 0)

    lax.fori_loop(0, tiles, tile, 0)
    across = images if straight else LANES
    count = images // across

    def block(n, _):
        lane = pl.ds(pl.multiple_of(lax.rem(n, count) * across, LANES), across)
        j = pl.multiple_of(n // count * 8, 8)
        cosine_terms = [terms[pl.ds(m * rows + j, 8), lane] for m in range(ORDERS)]
        sine_terms = [terms[pl.ds(m * rows + share + j, 8), lane] for m in range(ORDERS)]
        best[pl.ds(j, 8), lane] = best_angle(cosine_terms, sine_terms)
        return 0

    lax.fori_loop(0, (share // 8) * count, block, 0)
    scale = math.sqrt(width) * scale_of(rows_ref[...]) * scale_ref[:1, :]
    return best[...] / scale


def first_kernel(rows_ref, turned_ref, order_ref, ends_ref, scale_ref, out_ref, best, pair, terms):
    out_ref[...] = round_scores(
        False, rows_ref, turned_ref, order_ref, ends_ref, scale_ref, best, pair, terms
    )


def last_kernel(before_ref, rows_ref, turned_ref, order_ref, ends_ref, scale_ref, out_ref, best, pair, terms):
    value = round_scores(True, rows_ref, turned_ref, order_ref, ends_ref, scale_ref, best, pair, terms)
    share, images = value.shape
    fill = jnp.zeros((LANES - ROUNDS * share, images), jnp.float32)
    later = ends_ref[ends_ref.shape[0] - 1] == 1
    both = [jnp.where(later, value, before_ref[...]), jnp.where(later, before_ref[...], value)]
    turned = jnp.transpose(jnp.concatenate([*both, fill], axis=0))
    lane = lax.broadcasted_iota(jnp.int32, (share // 2, LANES), 1)
    for g in range(images // share):
        top = turned[g * share : g * share + share // 2]
        low = pltpu.roll(turned[g * share + share // 2 : (g + 1) * share], LANES // 2, 1)
        out_ref[g] = jnp.where(lane < LANES // 2, top, low)


def place_kernel(pieces_ref, out_ref):
    count, short, _ = pieces_ref.shape
    share = 2 * short
    lane = lax.broadcasted_iota(jnp.int32, (short, LANES), 1)
    for r in range(ROUNDS):
        for h in range(2):
            for column in range(count * share // LANES):
                whole = None
                for k in range(LANES // share):
                    shift = (k * share - h * (LANES // 2) - r * share) % LANES
                    piece = pieces_ref[column * (LANES // share) + k]
                    piece = pltpu.roll(piece, shift, 1) if shift else piece
                    whole = piece if whole is None else jnp.where(lane < k * share, whole, piece)
                out_ref[r, h * short : (h + 1) * short, column * LANES : (column + 1) * LANES] = whole


VMEM = pl.BlockSpec(memory_space=pltpu.VMEM)
SMEM = pl.BlockSpec(memory_space=pltpu.SMEM)
HBM = pl.BlockSpec(memory_space=pltpu.HBM)


def call(kernel, inputs, shapes, in_specs=None, out_specs=None, scratch=(), flops=0):
    return pl.pallas_call(
        kernel,
        out_shape=shapes,
        in_specs=in_specs or [VMEM] * len(inputs),
        out_specs=out_specs or jax.tree.map(lambda _: VMEM, shapes),
        scratch_shapes=list(scratch),
        compiler_params=pltpu.CompilerParams(vmem_limit_bytes=32 * 2**20),
        cost_estimate=pl.CostEstimate(flops=flops, bytes_accessed=2**21, transcendentals=0),
    )(*inputs)


def from_chip(index, chips, rows, beside):
    def moved(apart):
        pairs = [(source, source ^ (2 * apart)) for source in range(2 * chips)]

        def branch(piece, *others):
            there = lax.ppermute(piece, "blk", pairs) if apart else piece
            return there, beside(*others)

        return branch

    return lax.switch(index, [moved(apart) for apart in range(chips)], *rows)


def per_device(coeffs, orders, plan):
    ang_count = lax.axis_size("ang")
    blocks = lax.axis_size("blk")
    images, width = coeffs.shape
    half = width // 2
    tiles = half // LANES
    share = images // ang_count
    f32, bf16, i32 = jnp.float32, jnp.bfloat16, jnp.int32
    shape = jax.ShapeDtypeStruct

    first, second, crossed, turned, own_rows, order, ends, scale = call(
        prepare_kernel,
        tuple(
            pltpu.with_memory_space_constraint(x, pltpu.HBM) for x in (coeffs, orders.reshape(1, half), plan)
        ),
        (
            shape((1,), i32),
            shape((1,), i32),
            shape((ROUNDS, width), i32),
            shape((width, images), bf16),
            shape((share, width), bf16),
            shape((1, width), i32),
            shape((2 * tiles + 1,), i32),
            shape((8, images), f32),
        ),
        [HBM, HBM, HBM],
        (SMEM, SMEM, VMEM, VMEM, VMEM, VMEM, SMEM, VMEM),
        [
            pltpu.VMEM((images, width), bf16),
            pltpu.VMEM((1, half), i32),
            pltpu.SMEM((ROUNDS,), i32),
            pltpu.VMEM((half, half), bf16),
            pltpu.VMEM((images, width), bf16),
            pltpu.SemaphoreType.DMA((3,)),
        ],
        flops=2 * images * width * half,
    )
    other_rows = lax.ppermute(own_rows, "blk", [(source, source ^ 1) for source in range(blocks)])
    sent = [jnp.where(crossed[r][None, :] != 0, other_rows, own_rows) for r in range(ROUNDS)]
    rows = 2 * share
    scratch = [
        pltpu.VMEM((share, images), f32),
        pltpu.VMEM((rows, width), bf16),
        pltpu.VMEM(((ORDERS + GROUP) * rows, images), f32),
    ]
    shared = (turned, order, ends, scale)
    flops = 2 * images * width * rows * 8

    def score_first(rows, *shared):
        return call(
            first_kernel,
            (rows, *shared),
            shape((share, images), f32),
            [VMEM, VMEM, VMEM, SMEM, VMEM],
            scratch=scratch,
            flops=flops,
        )

    rows_first, _ = from_chip(first[0], blocks // 2, (sent[0],), lambda: ())
    rows_second, before = from_chip(
        second[0], blocks // 2, (sent[1], rows_first, *shared), score_first
    )
    pieces = call(
        last_kernel,
        (before, rows_second, *shared),
        shape((ang_count, share // 2, LANES), f32),
        [VMEM, VMEM, VMEM, VMEM, SMEM, VMEM],
        scratch=scratch,
        flops=flops,
    )
    pieces = lax.all_to_all(pieces, "ang", 0, 0, tiled=True)
    return call(place_kernel, (pieces,), shape((ROUNDS, share, images), f32))


def solution(mesh):
    in_specs = (P("blk", None), P(), P())
    out_specs = P(None, ("blk", "ang"), None)
    return jax.shard_map(
        per_device, mesh=mesh, in_specs=in_specs, out_specs=out_specs, check_vma=False
    )
```

```python
import functools
import math

import jax
import jax.numpy as jnp
from jax import lax
from jax.experimental import pallas as pl
from jax.experimental.pallas import tpu as pltpu
from jax.sharding import PartitionSpec as P

ANGLES = 128
ORDERS = 48
ROUNDS = 2
LANES = 128
GROUP = 8
CHAINS = 4
KINDS = 64


def plus(u, v):
    if u is None or v is None:
        return u if v is None else v
    (su, a), (sv, b) = u, v
    if su == sv:
        return (su, a + b)
    return (1, a - b) if su > 0 else (1, b - a)


def negative(u):
    return None if u is None else (-u[0], u[1])


def minus(u, v):
    return plus(u, negative(v))


def times(u, factor):
    return None if u is None else (u[0], u[1] * jnp.float32(factor))


def plain(u):
    return u[1] if u[0] > 0 else -u[1]


def cosine_sums(x):
    size = len(x)
    if size == 1:
        return [x[0]]
    half = size // 2
    even = cosine_sums([plus(x[n], x[size - 1 - n]) for n in range(half)])
    odd = cosine_sums(
        [
            times(minus(x[n], x[size - 1 - n]), 2.0 * math.cos(math.pi * (2 * n + 1) / (2 * size)))
            for n in range(half)
        ]
    )
    out = [None] * size
    for a in range(half):
        out[2 * a] = even[a]
        out[2 * a + 1] = times(odd[0], 0.5) if a == 0 else minus(odd[a], out[2 * a - 1])
    return out


def padded(x, size):
    return x + [None] * (size - len(x))


def cosine_series(terms, period):
    if len(terms) == 1:
        return [terms[0]] * (period // 2 + 1)
    quarter = period // 4
    even = cosine_series(terms[0::2], period // 2)
    odd = cosine_sums(padded(terms[1::2], quarter)) + [None]
    out = [None] * (period // 2 + 1)
    for a in range(quarter + 1):
        out[a] = plus(even[a], odd[a])
        out[period // 2 - a] = minus(even[a], odd[a])
    return out


def sine_series(terms, period):
    if len(terms) == 1:
        return [None] * (period // 2 + 1)
    quarter = period // 4
    even = sine_series(terms[0::2], period // 2)
    flipped = [u if n % 2 == 0 else negative(u) for n, u in enumerate(terms[1::2])]
    odd = [None] + cosine_sums(padded(flipped, quarter))[::-1]
    out = [None] * (period // 2 + 1)
    for a in range(quarter + 1):
        out[period // 2 - a] = minus(odd[a], even[a])
        out[a] = plus(even[a], odd[a])
    return out


def best_angle(cosine_terms, sine_terms):
    across = cosine_series([(1, u) for u in cosine_terms], ANGLES)
    along = sine_series([(1, u) for u in sine_terms], ANGLES)
    best = [None] * CHAINS
    for n, (u, v) in enumerate(zip(across, along, strict=True)):
        value = plain(u)
        if v is not None:
            value = value + jnp.abs(v[1])
        k = n % CHAINS
        best[k] = value if best[k] is None else jnp.maximum(best[k], value)
    return functools.reduce(jnp.maximum, best)


def scale_of(rows):
    wide = rows.astype(jnp.float32)
    return jnp.sqrt(jnp.mean(wide * wide, axis=1, keepdims=True) + 1e-06)


def reach_of(offset):
    chip = lax.shift_right_logical(offset, 1)
    return jnp.where(chip == 0, 0, jnp.where((chip & 6) == 0, 1, 2))


def prepare_kernel(
    own_hbm, orders_hbm, plan_hbm, first_ref, second_ref, crossed_ref, turned_ref, rows_ref, order_ref, ends_ref, scale_ref,
    own, orders, plan, select, gathered, arrived
):
    half = orders.shape[1]
    images = own.shape[0]
    share = rows_ref.shape[0]
    tiles = half // LANES
    copies = [
        pltpu.make_async_copy(source, target, arrived.at[n])
        for n, (source, target) in enumerate(((orders_hbm, orders), (plan_hbm, plan), (own_hbm, own)))
    ]
    for copy in copies:
        copy.start()
    copies[0].wait()
    row = lax.broadcasted_iota(jnp.int32, (LANES, 2 * LANES), 0)
    column = lax.broadcasted_iota(jnp.int32, (LANES, 2 * LANES), 1)
    earlier = jnp.where((row < column) | (column >= LANES), 1.0, 0.0).astype(jnp.bfloat16)
    which = lax.broadcasted_iota(jnp.int32, (KINDS, half), 0)
    count = jnp.sum(jnp.where(orders[...] < which, 1.0, 0.0), axis=1, keepdims=True)
    spot = lax.broadcasted_iota(jnp.int32, (KINDS, half), 1).astype(jnp.float32)
    begun = jnp.where((count <= spot) & (which > 0), 1.0, 0.0)
    order = jnp.sum(begun, axis=0, keepdims=True).astype(jnp.int32)
    count = jnp.broadcast_to(count, (KINDS, LANES))
    same = jnp.where(orders[...] == which, 1.0, 0.0)
    places = []
    for c in range(tiles):
        part = same[:, c * LANES : (c + 1) * LANES]
        found = jnp.dot(part.astype(jnp.bfloat16), earlier, preferred_element_type=jnp.float32)
        places.append(jnp.sum(part * (count + found[:, :LANES]), axis=0, keepdims=True))
        count = count + found[:, LANES:]
    place = jnp.concatenate(places, axis=1)
    place = jnp.transpose(jnp.broadcast_to(place, (LANES, half))).astype(jnp.int32)
    spot = lax.broadcasted_iota(jnp.int32, (LANES, half), 1)
    for c in range(tiles):
        rows = slice(c * LANES, (c + 1) * LANES)
        select[rows, :] = jnp.where(spot == place[rows, :1], 1.0, 0.0).astype(jnp.bfloat16)
    for t in range(tiles):
        part = order[:, t * LANES : (t + 1) * LANES]
        order_ref[:, 2 * t * LANES : (2 * t + 1) * LANES] = part
        order_ref[:, (2 * t + 1) * LANES : (2 * t + 2) * LANES] = part
        ends_ref[2 * t] = jnp.min(part)
        ends_ref[2 * t + 1] = jnp.max(part)
    copies[1].wait()
    later = (reach_of(plan[0]) > reach_of(plan[1])).astype(jnp.int32)
    ends_ref[2 * tiles] = later
    for r, ref in enumerate((first_ref, second_ref)):
        offset = jnp.where(later == r, plan[0], plan[1])
        ref[0] = lax.shift_right_logical(offset, 1)
        crossed_ref[r : r + 1, :] = jnp.full((1, 2 * half), offset & 1, jnp.int32)
    copies[2].wait()
    for side in range(2):
        moved = jnp.dot(
            own[:, side * half : (side + 1) * half], select[...], preferred_element_type=jnp.float32
        ).astype(jnp.bfloat16)
        for t in range(tiles):
            there = slice((2 * t + side) * LANES, (2 * t + side + 1) * LANES)
            part = moved[:, t * LANES : (t + 1) * LANES]
            gathered[:, there] = part
            turned_ref[there, :] = jnp.transpose(part)
    mine = pl.ds(pl.multiple_of(lax.axis_index("ang") * share, share), share)
    rows_ref[...] = gathered[mine, :]
    scale_ref[...] = jnp.transpose(jnp.broadcast_to(scale_of(own[...]), (images, LANES)))[:8]


def tile_terms(cols, base, order_ref, turned_ref, pair):
    here, block = order_ref[:, cols], pair[:, cols]
    masked = jnp.concatenate(
        [block * jnp.where(here == base + q, 1.0, 0.0).astype(jnp.bfloat16) for q in range(GROUP)], axis=0
    )
    return jnp.dot(masked, turned_ref[cols, :], preferred_element_type=jnp.float32)


def clear_terms(terms, rows, first, last):
    def clear(m, _):
        terms[pl.ds(pl.multiple_of(m * rows, rows), rows), :] = jnp.zeros((rows, terms.shape[1]), jnp.float32)
        return 0

    lax.fori_loop(first, last, clear, 0)


def round_scores(straight, rows_ref, turned_ref, order_ref, ends_ref, scale_ref, best, pair, terms):
    share, width = rows_ref.shape
    images = turned_ref.shape[1]
    tiles = width // (2 * LANES)
    rows = 2 * share
    def couple(t, _):
        one = pl.ds(pl.multiple_of(2 * t * LANES, LANES), LANES)
        two = pl.ds(pl.multiple_of((2 * t + 1) * LANES, LANES), LANES)
        x, y = rows_ref[:, one], rows_ref[:, two]
        pair[:share, one] = x
        pair[:share, two] = y
        pair[share:, one] = y
        pair[share:, two] = -x
        return 0

    lax.fori_loop(0, tiles, couple, 0)

    if straight:
        reach = 0
        for t in range(tiles):
            clear_terms(terms, rows, reach, ends_ref[2 * t])
            reach = ends_ref[2 * t] + GROUP
        clear_terms(terms, rows, reach, ORDERS)
        for t in range(tiles):
            cols = slice(2 * t * LANES, (2 * t + 2) * LANES)
            base = ends_ref[2 * t]
            found = tile_terms(cols, base, order_ref, turned_ref, pair)
            first = pl.ds(pl.multiple_of(base * rows, rows), rows)
            after = pl.ds(pl.multiple_of((base + 1) * rows, rows), (GROUP - 1) * rows)
            if t == 0:
                terms[first, :] = found[:rows]
            else:
                written = base < ends_ref[2 * t - 2] + GROUP
                terms[first, :] = found[:rows] + jnp.where(written, terms[first, :], 0.0)
            terms[after, :] = found[rows:]
    else:
        clear_terms(terms, rows, 0, ORDERS + GROUP)

    def tile(t, _):
        least, most = ends_ref[2 * t], ends_ref[2 * t + 1]
        cols = pl.ds(pl.multiple_of(2 * t * LANES, 2 * LANES), 2 * LANES)

        def step(c, _):
            base = least + GROUP * c
            at = pl.ds(pl.multiple_of(base * rows, rows), GROUP * rows)
            terms[at, :] += tile_terms(cols, base, order_ref, turned_ref, pair)
            return 0

        return lax.fori_loop(1 if straight else 0, (most - least) // GROUP + 1, step, 0)

    lax.fori_loop(0, tiles, tile, 0)
    across = images if straight else LANES
    count = images // across

    def block(n, _):
        lane = pl.ds(pl.multiple_of(lax.rem(n, count) * across, LANES), across)
        j = pl.multiple_of(n // count * 8, 8)
        cosine_terms = [terms[pl.ds(m * rows + j, 8), lane] for m in range(ORDERS)]
        sine_terms = [terms[pl.ds(m * rows + share + j, 8), lane] for m in range(ORDERS)]
        best[pl.ds(j, 8), lane] = best_angle(cosine_terms, sine_terms)
        return 0

    lax.fori_loop(0, (share // 8) * count, block, 0)
    scale = math.sqrt(width) * scale_of(rows_ref[...]) * scale_ref[:1, :]
    return best[...] / scale


def first_kernel(rows_ref, turned_ref, order_ref, ends_ref, scale_ref, out_ref, best, pair, terms):
    out_ref[...] = round_scores(
        False, rows_ref, turned_ref, order_ref, ends_ref, scale_ref, best, pair, terms
    )


def last_kernel(before_ref, rows_ref, turned_ref, order_ref, ends_ref, scale_ref, out_ref, best, pair, terms):
    value = round_scores(True, rows_ref, turned_ref, order_ref, ends_ref, scale_ref, best, pair, terms)
    share, images = value.shape
    fill = jnp.zeros((LANES - ROUNDS * share, images), jnp.float32)
    later = ends_ref[ends_ref.shape[0] - 1] == 1
    both = [jnp.where(later, value, before_ref[...]), jnp.where(later, before_ref[...], value)]
    turned = jnp.transpose(jnp.concatenate([*both, fill], axis=0))
    lane = lax.broadcasted_iota(jnp.int32, (share // 2, LANES), 1)
    for g in range(images // share):
        top = turned[g * share : g * share + share // 2]
        low = pltpu.roll(turned[g * share + share // 2 : (g + 1) * share], LANES // 2, 1)
        out_ref[g] = jnp.where(lane < LANES // 2, top, low)


def place_kernel(pieces_ref, out_ref):
    count, short, _ = pieces_ref.shape
    share = 2 * short
    lane = lax.broadcasted_iota(jnp.int32, (short, LANES), 1)
    for r in range(ROUNDS):
        for h in range(2):
            for column in range(count * share // LANES):
                whole = None
                for k in range(LANES // share):
                    shift = (k * share - h * (LANES // 2) - r * share) % LANES
                    piece = pieces_ref[column * (LANES // share) + k]
                    piece = pltpu.roll(piece, shift, 1) if shift else piece
                    whole = piece if whole is None else jnp.where(lane < k * share, whole, piece)
                out_ref[r, h * short : (h + 1) * short, column * LANES : (column + 1) * LANES] = whole


VMEM = pl.BlockSpec(memory_space=pltpu.VMEM)
SMEM = pl.BlockSpec(memory_space=pltpu.SMEM)
HBM = pl.BlockSpec(memory_space=pltpu.HBM)


def call(kernel, inputs, shapes, in_specs=None, out_specs=None, scratch=(), flops=0):
    return pl.pallas_call(
        kernel,
        out_shape=shapes,
        in_specs=in_specs or [VMEM] * len(inputs),
        out_specs=out_specs or jax.tree.map(lambda _: VMEM, shapes),
        scratch_shapes=list(scratch),
        compiler_params=pltpu.CompilerParams(vmem_limit_bytes=32 * 2**20),
        cost_estimate=pl.CostEstimate(flops=flops, bytes_accessed=2**21, transcendentals=0),
    )(*inputs)


def from_chip(index, chips, rows, beside):
    def moved(apart):
        pairs = [(source, source ^ (2 * apart)) for source in range(2 * chips)]

        def branch(piece, *others):
            there = lax.ppermute(piece, "blk", pairs) if apart else piece
            return there, beside(*others)

        return branch

    return lax.switch(index, [moved(apart) for apart in range(chips)], *rows)


def per_device(coeffs, orders, plan):
    ang_count = lax.axis_size("ang")
    blocks = lax.axis_size("blk")
    images, width = coeffs.shape
    half = width // 2
    tiles = half // LANES
    share = images // ang_count
    f32, bf16, i32 = jnp.float32, jnp.bfloat16, jnp.int32
    shape = jax.ShapeDtypeStruct

    first, second, crossed, turned, own_rows, order, ends, scale = call(
        prepare_kernel,
        tuple(
            pltpu.with_memory_space_constraint(x, pltpu.HBM) for x in (coeffs, orders.reshape(1, half), plan)
        ),
        (
            shape((1,), i32),
            shape((1,), i32),
            shape((ROUNDS, width), i32),
            shape((width, images), bf16),
            shape((share, width), bf16),
            shape((1, width), i32),
            shape((2 * tiles + 1,), i32),
            shape((8, images), f32),
        ),
        [HBM, HBM, HBM],
        (SMEM, SMEM, VMEM, VMEM, VMEM, VMEM, SMEM, VMEM),
        [
            pltpu.VMEM((images, width), bf16),
            pltpu.VMEM((1, half), i32),
            pltpu.SMEM((ROUNDS,), i32),
            pltpu.VMEM((half, half), bf16),
            pltpu.VMEM((images, width), bf16),
            pltpu.SemaphoreType.DMA((3,)),
        ],
        flops=2 * images * width * half,
    )
    other_rows = lax.ppermute(own_rows, "blk", [(source, source ^ 1) for source in range(blocks)])
    sent = [jnp.where(crossed[r][None, :] != 0, other_rows, own_rows) for r in range(ROUNDS)]
    rows = 2 * share
    scratch = [
        pltpu.VMEM((share, images), f32),
        pltpu.VMEM((rows, width), bf16),
        pltpu.VMEM(((ORDERS + GROUP) * rows, images), f32),
    ]
    shared = (turned, order, ends, scale)
    flops = 2 * images * width * rows * 8

    def score_first(rows, *shared):
        return call(
            first_kernel,
            (rows, *shared),
            shape((share, images), f32),
            [VMEM, VMEM, VMEM, SMEM, VMEM],
            scratch=scratch,
            flops=flops,
        )

    rows_first, _ = from_chip(first[0], blocks // 2, (sent[0],), lambda: ())
    rows_second, before = from_chip(
        second[0], blocks // 2, (sent[1], rows_first, *shared), score_first
    )
    pieces = call(
        last_kernel,
        (before, rows_second, *shared),
        shape((ang_count, share // 2, LANES), f32),
        [VMEM, VMEM, VMEM, VMEM, SMEM, VMEM],
        scratch=scratch,
        flops=flops,
    )
    pieces = lax.all_to_all(pieces, "ang", 0, 0, tiled=True)
    return call(place_kernel, (pieces,), shape((ROUNDS, share, images), f32))


def solution(mesh):
    in_specs = (P("blk", None), P(), P())
    out_specs = P(None, ("blk", "ang"), None)
    return jax.shard_map(
        per_device, mesh=mesh, in_specs=in_specs, out_specs=out_specs, check_vma=False
    )
```
